32 devices in a mesh: trial: 8 (over z, core), slab: 2 (over y), freq: 2 (over x).
Axes of the slice: x: 2, y: 2, z: 4, core: 2. Of those that a mesh axis runs over, the one named last changes fastest.
Arguments:
- orbitals: float32 [8, 8, 64, 128], P('trial', 'slab'), may hold values from -6 to 6
- energies: float32 [8], P('trial'), may hold values from 0 to 1
- potential: float32 [8, 64, 128], P('slab'), may hold values from 0 to 1
- trials: float32 [64, 8, 64, 128], P('trial', 'slab'), may hold values from -6 to 6
- cheb: float32 [2, 4], P('freq'), may hold values from 0.3 to 1
- shifts: float32 [2], P('freq'), may hold values from -0.5 to 0.5
- column_order: int32 [64], replicated, may hold values from 0 to 63, each once
Outputs:
- gram: float32 [64, 64], P(('trial', 'slab'))
The draws below stay inside these ranges and needn't reach their ends.
Inputs may be any that keep to these rules, and one draw needn't show every extreme that they name: `column_order`: each of 0 to 63 appears once.
All inputs are finite; a program needn't handle non-finite values.
Results may differ from the reference program's by a relative error of at most 0.00024.
Values sent between devices are 32-bit elements; how exact they have to be, the bound alone decides.
A program may use at most 64 MiB of HBM per device.

```python
import math
import jax
import jax.numpy as jnp
from jax import lax

NY = 64
NZ = 128
KSTEPS = 3
FREQS = 2
TRIALS = 64
NORB = 8
NX = 8


def plane_profile(key, rows):
    phase = jax.random.uniform(key, (rows, 1), jnp.float32, -math.pi, math.pi)
    plane = jnp.arange(NX).astype(jnp.float32)
    profile = 1.0 + 0.3 * jnp.sin(2.0 * math.pi * plane[None] / NX + phase)
    return profile[:, :, None, None]


def draw_orbitals(key, part):
    key_phase = jax.random.fold_in(key, 11)
    key_column = jax.random.fold_in(key, 12)
    key_rough = jax.random.fold_in(key, 13)
    profile = plane_profile(key_phase, NORB)
    column = jnp.clip(jax.random.normal(key_column, (NORB, 1, NY, NZ), jnp.float32), -2.5, 2.5)
    rough = 0.7 * jnp.clip(jax.random.normal(key_rough, (NORB, NX, NY, NZ), jnp.float32), -3.0, 3.0)
    return (profile * column + rough).astype(jnp.float32)


def draw_trials(key, part):
    key_phase = jax.random.fold_in(key, 21)
    key_column = jax.random.fold_in(key, 22)
    key_rough = jax.random.fold_in(key, 23)
    profile = plane_profile(key_phase, TRIALS)
    column = jnp.clip(jax.random.normal(key_column, (TRIALS, 1, NY, NZ), jnp.float32), -2.5, 2.5)
    rough = 0.7 * jnp.clip(jax.random.normal(key_rough, (TRIALS, NX, NY, NZ), jnp.float32), -3.0, 3.0)
    return (profile * column + rough).astype(jnp.float32)


def level_of(key, extent, split, smallest, high):
    factor_of = 1.0
    for position, shards_of in split:
        heights = jax.random.uniform(jax.random.fold_in(jax.random.fold_in(key, 6), position), (shards_of,), jnp.float32, smallest / len(split), high / len(split))
        factor_of = factor_of * jnp.repeat(jnp.exp(heights), extent[position] // shards_of).reshape((-1,) + (1,) * (len(extent) - 1 - position))
    return factor_of


def setup_inputs(seed: int = 0) -> dict:
    key_list = jax.random.split(jax.random.key(seed), 8)
    orbitals = draw_orbitals(jax.random.fold_in(key_list[7], 71), 0)
    energies = jnp.clip(1.0 * jax.random.uniform(key_list[1], (NORB,), jnp.float32) ** level_of(key_list[1], (NORB,), ((0, 8),), -0.2, 0.2), 0.0, 1.0)
    potential = jnp.clip(1.0 * jax.random.uniform(key_list[2], (NX, NY, NZ), jnp.float32) ** level_of(key_list[2], (NX, NY, NZ), ((0, 2),), -0.2, 0.2), 0.0, 1.0)
    trials = draw_trials(jax.random.fold_in(key_list[7], 71), 0)
    cheb = jnp.clip(0.3 + 0.7 * jax.random.uniform(key_list[4], (FREQS, KSTEPS + 1), jnp.float32) ** level_of(key_list[4], (FREQS, KSTEPS + 1), ((0, 2),), -0.2, 0.2), 0.3, 1.0)
    shifts = jnp.clip(jax.random.uniform(key_list[5], (FREQS,), jnp.float32, -0.5, 0.5) * level_of(key_list[5], (FREQS,), ((0, 2),), -0.4, 0.0), -0.5, 0.5)
    column_order = jax.random.permutation(key_list[6], TRIALS).astype(jnp.int32)
    return {"orbitals": orbitals, "energies": energies, "potential": potential, "trials": trials, "cheb": cheb, "shifts": shifts, "column_order": column_order}


def apply_op(field, coef):
    padded = jnp.pad(field, ((0, 0), (1, 1), (1, 1), (1, 1)))
    beside = padded[:, 2:, 1:-1, 1:-1] + padded[:, :-2, 1:-1, 1:-1]
    beside = beside + padded[:, 1:-1, 2:, 1:-1] + padded[:, 1:-1, :-2, 1:-1]
    beside = beside + padded[:, 1:-1, 1:-1, 2:] + padded[:, 1:-1, 1:-1, :-2]
    return (coef[None] * field - 0.5 * beside) / 4.5

def reference(orbitals, energies, potential, trials, cheb, shifts, column_order):
    norb = orbitals.shape[0]

    def one_orbital(carry, item):
        orbital, energy = item
        start = orbital[None] * trials
        parts = []
        for freq in range(FREQS):
            coef = potential - energy - shifts[freq]
            before = start
            now = apply_op(start, coef)
            response = cheb[freq, 0] * start + cheb[freq, 1] * now
            for order in range(2, KSTEPS + 1):
                after = 2.0 * apply_op(now, coef) - before
                response = response + cheb[freq, order] * after
                before, now = (now, after)
            parts.append(orbital[None] * response)
        return (carry + jnp.stack(parts), None)
    empty = jnp.zeros((FREQS, TRIALS, NX, NY, NZ), jnp.float32)
    density, _ = lax.scan(one_orbital, empty, (orbitals, energies))
    total = lax.optimization_barrier(jnp.sum(density, axis=0))
    left = trials.reshape(TRIALS, -1)[column_order]
    right = total.reshape(TRIALS, -1)[column_order]
    gram = jnp.dot(left, right.T, precision=lax.Precision.HIGHEST, preferred_element_type=jnp.float32)
    return gram / jnp.sqrt(jnp.float32(NX * NY * NZ * norb))
```

```python
import functools

import jax
import jax.numpy as jnp
from jax import lax
from jax.experimental import pallas as pl
from jax.experimental.pallas import tpu as pltpu
from jax.sharding import PartitionSpec as P

REACH = 3
MESH = pl.DeviceIdType.MESH
HIGH = lax.Precision.HIGHEST

OFFSETS = [
    (dx, dy, dz)
    for dz in range(-REACH, REACH + 1)
    for dx in range(REACH + 1)
    for dy in range(-REACH, REACH + 1)
    if abs(dx) + abs(dy) + abs(dz) <= REACH and (dx, dy, dz) >= (0, 0, 0)
]
PATHS = {(1, 1, 1): 6.0, (0, 1, 2): 3.0, (0, 0, 3): 1.0}


def rolled(value, shift):
    shift = shift % value.shape[1]
    return value if shift == 0 else pltpu.roll(value, shift, 1)


def kernel(
    sizes, orb, par, pot, tri, order, out,
    orbs, wide, pots, pars, freqs, scaled, weights, coefs, dens, rho_in, tri_in, rows_out, rows_in,
    near_s, near_r, orb_s, orb_r, pass_s, pass_r, par_s, par_r, frq_s, frq_r,
    tri_s, tri_r, rho_s, rho_r, row_s, row_r, loc,
):
    nt, ns, nf = sizes
    per, planes, ny, nz = tri.shape
    norb = orbs.shape[0]
    half = ny // nf
    window = half + 8
    total = nt * per
    piece = planes * half // nt
    t, s, f = lax.axis_index("trial"), lax.axis_index("slab"), lax.axis_index("freq")
    mate = t + 1 - 2 * lax.rem(t, 2)
    src_y = pl.ds(pl.multiple_of(f * (half - 8), 8), window)
    dst_y = pl.ds(pl.multiple_of(8 - 8 * f, 8), window)
    edge_y = pl.ds(pl.multiple_of(f * window, 8), 8)
    last = s == ns - 1

    orbs[:, :, edge_y, :] = jnp.zeros((norb, planes + REACH, 8, nz), jnp.float32)
    wide[:, :, edge_y, :] = jnp.zeros((per, planes + REACH, 8, nz), jnp.float32)
    pots[:, edge_y, :] = jnp.zeros((planes + REACH + 1, 8, nz), jnp.float32)

    @pl.when(last)
    def _():
        orbs[t, planes:, dst_y, :] = jnp.zeros((REACH, window, nz), jnp.float32)
        wide[:, planes:, dst_y, :] = jnp.zeros((per, REACH, window, nz), jnp.float32)
        pots[planes + 1 :, dst_y, :] = jnp.zeros((REACH, window, nz), jnp.float32)

    @pl.when(s == 0)
    def _():
        pots[0, dst_y, :] = jnp.zeros((window, nz), jnp.float32)

    locals_ = [
        pltpu.make_async_copy(orb.at[0, :, src_y, :], orbs.at[t, :planes, dst_y, :], loc.at[0]),
        pltpu.make_async_copy(tri.at[:, :, src_y, :], wide.at[:, :planes, dst_y, :], loc.at[1]),
        pltpu.make_async_copy(pot.at[:, src_y, :], pots.at[1 : planes + 1, dst_y, :], loc.at[2]),
        pltpu.make_async_copy(par, pars.at[t], loc.at[3]),
        pltpu.make_async_copy(par, freqs.at[f], loc.at[4]),
    ]
    for copy in locals_:
        copy.start()

    def device(k):
        dt, ds, df = k // (ns * nf), (k // nf) % ns, k % nf
        return lax.rem(t + dt, nt), lax.rem(s + ds, ns), lax.rem(f + df, nf)

    count = nt * ns * nf
    barrier = pltpu.get_barrier_semaphore()

    if count <= 64:
        for k in range(1, count):
            pt, ps, pf = device(k)
            pl.semaphore_signal(barrier, inc=1, device_id={"trial": pt, "slab": ps, "freq": pf}, device_id_type=MESH)
    else:

        @pl.loop(1, count)
        def _(k):
            pt, ps, pf = device(k)
            pl.semaphore_signal(barrier, inc=1, device_id={"trial": pt, "slab": ps, "freq": pf}, device_id_type=MESH)

    pl.semaphore_wait(barrier, count - 1)

    def remote(src, dst, send, recv, **where):
        return pltpu.make_async_remote_copy(
            src_ref=src, dst_ref=dst, send_sem=send, recv_sem=recv, device_id=where, device_id_type=MESH
        )

    below, above = jnp.maximum(s - 1, 0), jnp.minimum(s + 1, ns - 1)
    down = [
        remote(orb.at[0, :REACH, src_y, :], orbs.at[t, planes:, dst_y, :], near_s.at[0], near_r.at[0], slab=below),
        remote(tri.at[:, :REACH, src_y, :], wide.at[:, planes:, dst_y, :], near_s.at[1], near_r.at[1], slab=below),
        remote(pot.at[:REACH, src_y, :], pots.at[planes + 1 :, dst_y, :], near_s.at[2], near_r.at[2], slab=below),
    ]
    up = remote(pot.at[planes - 1, src_y, :], pots.at[0, dst_y, :], near_s.at[3], near_r.at[3], slab=above)

    @pl.when(s > 0)
    def _():
        down[0].start()
        down[2].start()
        down[1].start()

    @pl.when(s < ns - 1)
    def _():
        up.start()

    par_copies = []
    for j in range(1, nt):
        par_copies.append(remote(par, pars.at[t], par_s.at[j], par_r.at[j], trial=lax.rem(t + j, nt)))
    for j in range(1, nf):
        par_copies.append(remote(par, freqs.at[f], frq_s.at[j], frq_r.at[j], freq=lax.rem(f + j, nf)))
    for copy in par_copies:
        copy.start()

    for copy in locals_:
        copy.wait()

    @pl.when(s < ns - 1)
    def _():
        down[0].wait_recv()

    def block(slot):
        return orbs.at[slot, :, dst_y, :]

    chips = nt // 2
    orb_copies = []
    for j in range(1, chips):
        orb_copies.append(remote(block(t), block(t), orb_s.at[j], orb_r.at[j], trial=lax.rem(t + 2 * j, nt)))
    pass_copies = [remote(block(t), block(t), pass_s.at[0], pass_r.at[0], trial=mate)]
    for copy in orb_copies + pass_copies:
        copy.start()

    tri_copies = []
    span = half // piece
    for j in range(1, nt):
        peer = lax.rem(t + j, nt)
        y0 = pl.multiple_of(f * half + lax.rem(peer, span) * piece, 8)
        part = tri.at[:, peer // span, pl.ds(y0, piece), :]
        tri_copies.append(remote(part, tri_in.at[t], tri_s.at[j], tri_r.at[j], trial=peer))
    for copy in tri_copies:
        copy.start()
    y0 = pl.multiple_of(f * half + lax.rem(t, span) * piece, 8)
    own_tri = pltpu.make_async_copy(tri.at[:, t // span, pl.ds(y0, piece), :], tri_in.at[t], loc.at[5])
    own_tri.start()

    for j in range(1, chips):
        orb_copies[j - 1].wait_recv()
        source = lax.rem(t - 2 * j + nt, nt)
        copy = remote(block(source), block(source), pass_s.at[j], pass_r.at[j], trial=mate)
        copy.start()
        pass_copies.append(copy)
    for copy in par_copies:
        copy.wait_recv()

    inverse = 1.0 / 4.5
    hop = -0.5 / 4.5
    for i in range(norb):
        energy = pars[i, 0:1, :]
        terms = [0.0, 0.0, 0.0, 0.0]
        for w in range(nf):
            mu = (energy + freqs[w, 5:6, :]) * inverse
            c0, c1, c2, c3 = (freqs[w, 1 + n : 2 + n, :] for n in range(4))
            b0, b1, b2, b3 = c0 - c2, c1 - 3.0 * c3, 2.0 * c2, 4.0 * c3
            terms[0] += b0 - mu * (b1 - mu * (b2 - mu * b3))
            terms[1] += b1 - mu * (2.0 * b2 - 3.0 * mu * b3)
            terms[2] += b2 - 3.0 * mu * b3
            terms[3] += b3
        for n in range(4):
            weights[n, i] = jnp.broadcast_to(terms[n], weights.shape[2:])

    @pl.when(s < ns - 1)
    def _():
        down[1].wait_recv()
        down[2].wait_recv()

    @pl.when(s > 0)
    def _():
        up.wait_recv()

    for copy in pass_copies:
        copy.wait_recv()

    mid = slice(8, 8 + half)
    lane = lax.broadcasted_iota(jnp.int32, (half, nz), 1)
    row = lax.broadcasted_iota(jnp.int32, (half, nz), 0) + f * half

    def links(position, size):
        return (position >= 1).astype(jnp.float32) + (position + 1 < size).astype(jnp.float32)

    def one_plane(x, carry):
        xg = s * planes + x
        column = jnp.zeros((half, nz), jnp.int32) + xg
        for dz in range(-REACH, REACH + 1):
            group = [(n, off) for n, off in enumerate(OFFSETS) if off[2] == dz]
            if not group:
                continue
            depth = lane - dz
            inside = ((depth >= 0) & (depth < nz)).astype(jnp.float32)
            deepest = max(sum(map(abs, off)) for _, off in group)
            least = min(sum(map(abs, off)) for _, off in group)

            def prepare(i, carry):
                centre = rolled(orbs[i, x, mid, :], dz) * inside
                for n in range(least, 4):
                    scaled[n, i] = weights[n, i, 0:1, :] * centre
                return carry

            lax.fori_loop(0, norb, prepare, 0, unroll=True)

            def local(a, b, c):
                return rolled(pots[1 + x + a, 8 + b : 8 + b + half, :], dz - c) * inverse

            for index, (dx, dy, _) in group:
                steps = abs(dx) + abs(dy) + abs(dz)
                sums = {n: 0.0 for n in range(steps, 4)}
                for i in range(norb):
                    there = orbs[i, x + dx, 8 + dy : 8 + dy + half, :]
                    for n in sums:
                        sums[n] = sums[n] + scaled[n, i] * there
                if steps == 3:
                    kind = tuple(sorted(map(abs, (dx, dy, dz))))
                    coef = (PATHS[kind] * hop**3) * sums[3]
                elif steps == 2:
                    here, end = local(0, 0, 0), local(dx, dy, dz)
                    corners = [c for c in ((dx, 0, 0), (0, dy, 0), (0, 0, dz)) if c != (0, 0, 0)]
                    if len(corners) == 1:
                        middle = local(dx // 2, dy // 2, dz // 2)
                        coef = hop**2 * (sums[2] + (here + middle + end) * sums[3])
                    else:
                        middle = local(*corners[0]) + local(*corners[1])
                        coef = hop**2 * (2.0 * sums[2] + (2.0 * (here + end) + middle) * sums[3])
                elif steps == 1:
                    here, end = local(0, 0, 0), local(dx, dy, dz)
                    at = (column, row, depth)
                    size = (planes * ns, ny, nz)
                    move = (dx, dy, dz)
                    side, along = 0.0, 0.0
                    for axis in range(3):
                        if move[axis]:
                            along = links(at[axis], size[axis]) + links(at[axis] + move[axis], size[axis])
                        else:
                            side = side + links(at[axis], size[axis])
                    walks = along + 3.0 * side - 1.0
                    cubic = here * here + here * end + end * end + hop**2 * walks
                    coef = hop * (sums[1] + (here + end) * sums[2] + cubic * sums[3])
                else:
                    here = local(0, 0, 0)
                    degree = links(column, planes * ns) + links(row, ny) + links(lane, nz)
                    near = local(1, 0, 0) + local(-1, 0, 0) + local(0, 1, 0) + local(0, -1, 0)
                    near = near + jnp.where(lane + 1 < nz, local(0, 0, 1), 0.0)
                    near = near + jnp.where(lane >= 1, local(0, 0, -1), 0.0)
                    square = here * here + hop**2 * degree
                    cube = here * (here * here + 2.0 * hop**2 * degree) + hop**2 * near
                    coef = 0.5 * (sums[0] + here * sums[1] + square * sums[2] + cube * sums[3])
                coefs[index] = coef

        def one_trial(k, carry):
            density = 0.0
            for dz in range(-REACH, REACH + 1):
                group = [(n, off) for n, off in enumerate(OFFSETS) if off[2] == dz]
                if not group:
                    continue
                part = 0.0
                for index, (dx, dy, _) in group:
                    part = part + coefs[index] * wide[k, x + dx, 8 + dy : 8 + dy + half, :]
                density = density + rolled(part, -dz)
            for h in range(span):
                dens[x * span + h, k] = density[h * piece : (h + 1) * piece]
            return carry

        return lax.fori_loop(0, per, one_trial, carry)

    lax.fori_loop(0, planes, one_plane, 0)

    rho_copies = []
    for j in range(1, nt):
        peer = lax.rem(t + j, nt)
        rho_copies.append(remote(dens.at[peer], rho_in.at[t], rho_s.at[j], rho_r.at[j], trial=peer))
    for copy in rho_copies:
        copy.start()
    rho_in[t] = dens[t]
    own_tri.wait()
    for copy in tri_copies:
        copy.wait_recv()
    for copy in rho_copies:
        copy.wait_recv()

    contract = (((1,), (1,)), ((), ()))

    def dot(a, b):
        return lax.dot_general(a, b, contract, precision=HIGH, preferred_element_type=jnp.float32)

    gram = jnp.zeros((total, total), jnp.float32)
    for r in range(piece):
        left = tri_in[:, :, r, :].reshape(total, nz)
        right = rho_in[:, :, r, :].reshape(total, nz)
        gram = gram + dot(left, right) + dot(right, left)
    pick = (order[...] == lax.broadcasted_iota(jnp.int32, (total, total), 1)).astype(jnp.float32)
    half_way = jnp.dot(pick, gram, precision=HIGH, preferred_element_type=jnp.float32)
    factor = 1.0 / jnp.sqrt(jnp.float32(planes * ns * ny * nz * norb))
    final = dot(half_way, pick) * factor
    owned = total // (nt * ns)
    for r in range(nt * ns):
        rows_out[r] = final[r * owned : (r + 1) * owned]

    def me():
        return (t * ns + s) * nf + f

    def row_copy(k):
        pt, ps, pf = device(k)
        return remote(
            rows_out.at[pt * ns + ps], rows_in.at[me()], row_s.at[k], row_r.at[k], trial=pt, slab=ps, freq=pf
        )

    def each(action):
        if count <= 64:
            for k in range(1, count):
                action(k)
        else:
            pl.loop(1, count)(action)

    each(lambda k: row_copy(k).start())
    rows_in[me()] = rows_out[t * ns + s]
    each(lambda k: row_copy(k).wait())
    out[...] = jnp.sum(rows_in[...], axis=0)

    for copy in orb_copies + pass_copies + par_copies + tri_copies + rho_copies:
        copy.wait_send()

    @pl.when(s > 0)
    def _():
        for copy in down:
            copy.wait_send()

    @pl.when(s < ns - 1)
    def _():
        up.wait_send()


def local(sizes, orbitals, energies, potential, trials, cheb, shifts, column_order):
    nt, ns, nf = sizes
    per, planes, ny, nz = trials.shape
    norb = orbitals.shape[0] * nt
    half = ny // nf
    full = half + 16
    total = nt * per
    piece = planes * half // nt
    owned = total // (nt * ns)
    count = nt * ns * nf
    column = jnp.concatenate([energies, cheb[0], shifts, jnp.zeros((2,), jnp.float32)])
    par = jnp.broadcast_to(column[:, None], (8, 128))
    f32 = jnp.float32
    dma = pltpu.SemaphoreType.DMA
    anywhere = pl.BlockSpec(memory_space=pl.ANY)
    vmem = pl.BlockSpec(memory_space=pltpu.VMEM)
    return pl.pallas_call(
        functools.partial(kernel, sizes),
        out_shape=jax.ShapeDtypeStruct((owned, total), f32),
        in_specs=[anywhere, vmem, anywhere, anywhere, vmem],
        out_specs=vmem,
        scratch_shapes=[
            pltpu.VMEM((norb, planes + REACH, full, nz), f32),
            pltpu.VMEM((per, planes + REACH, full, nz), f32),
            pltpu.VMEM((planes + REACH + 1, full, nz), f32),
            pltpu.VMEM((nt, 8, 128), f32),
            pltpu.VMEM((nf, 8, 128), f32),
            pltpu.VMEM((4, norb, half, nz), f32),
            pltpu.VMEM((4, norb, 8, nz), f32),
            pltpu.VMEM((len(OFFSETS), half, nz), f32),
            pltpu.VMEM((nt, per, piece, nz), f32),
            pltpu.VMEM((nt, per, piece, nz), f32),
            pltpu.VMEM((nt, per, piece, nz), f32),
            pltpu.VMEM((nt * ns, owned, total), f32),
            pltpu.VMEM((count, owned, total), f32),
            dma((4,)), dma((4,)), dma((nt,)), dma((nt,)), dma((nt,)), dma((nt,)), dma((nt,)), dma((nt,)),
            dma((nf,)), dma((nf,)), dma((nt,)), dma((nt,)), dma((nt,)), dma((nt,)), dma((count,)), dma((count,)),
            dma((6,)),
        ],
        compiler_params=pltpu.CompilerParams(
            collective_id=0, has_side_effects=True, vmem_limit_bytes=48 * 1024 * 1024
        ),
    )(orbitals, par, potential, trials, column_order[:, None])


def solution(mesh):
    sizes = tuple(mesh.shape[name] for name in ("trial", "slab", "freq"))
    in_specs = (
        P("trial", "slab", None, None),
        P("trial"),
        P("slab", None, None),
        P("trial", "slab", None, None),
        P("freq", None),
        P("freq"),
        P(),
    )
    out_specs = P(("trial", "slab"), None)
    return jax.shard_map(
        functools.partial(local, sizes), mesh=mesh, in_specs=in_specs, out_specs=out_specs, check_vma=False
    )
```

```python
import functools

import jax
import jax.numpy as jnp
from jax import lax
from jax.experimental import pallas as pl
from jax.experimental.pallas import tpu as pltpu
from jax.sharding import PartitionSpec as P

REACH = 3
MESH = pl.DeviceIdType.MESH
HIGH = lax.Precision.HIGHEST

OFFSETS = [
    (dx, dy, dz)
    for dz in range(-REACH, REACH + 1)
    for dx in range(REACH + 1)
    for dy in range(-REACH, REACH + 1)
    if abs(dx) + abs(dy) + abs(dz) <= REACH and (dx, dy, dz) >= (0, 0, 0)
]
PATHS = {(1, 1, 1): 6.0, (0, 1, 2): 3.0, (0, 0, 3): 1.0}


def rolled(value, shift):
    shift = shift % value.shape[1]
    return value if shift == 0 else pltpu.roll(value, shift, 1)


def kernel(
    sizes, orb, par, pot, tri, order, out,
    orbs, wide, pots, pars, freqs, scaled, weights, coefs, dens, rho_in, tri_in, rows_out, rows_in,
    near_s, near_r, up_s, up_r, dn_s, dn_r, pass_s, pass_r, par_s, par_r, frq_s, frq_r,
    tri_s, tri_r, rho_s, rho_r, row_s, row_r, loc,
):
    nt, ns, nf = sizes
    per, planes, ny, nz = tri.shape
    norb = orbs.shape[0]
    half = ny // nf
    window = half + 8
    total = nt * per
    piece = planes * half // nt
    t, s, f = lax.axis_index("trial"), lax.axis_index("slab"), lax.axis_index("freq")
    mate = t + 1 - 2 * lax.rem(t, 2)
    src_y = pl.ds(pl.multiple_of(f * (half - 8), 8), window)
    dst_y = pl.ds(pl.multiple_of(8 - 8 * f, 8), window)
    edge_y = pl.ds(pl.multiple_of(f * window, 8), 8)
    last = s == ns - 1

    orbs[:, :, edge_y, :] = jnp.zeros((norb, planes + REACH, 8, nz), jnp.float32)
    wide[:, :, edge_y, :] = jnp.zeros((per, planes + REACH, 8, nz), jnp.float32)
    pots[:, edge_y, :] = jnp.zeros((planes + REACH + 1, 8, nz), jnp.float32)

    @pl.when(last)
    def _():
        orbs[t, planes:, dst_y, :] = jnp.zeros((REACH, window, nz), jnp.float32)
        wide[:, planes:, dst_y, :] = jnp.zeros((per, REACH, window, nz), jnp.float32)
        pots[planes + 1 :, dst_y, :] = jnp.zeros((REACH, window, nz), jnp.float32)

    @pl.when(s == 0)
    def _():
        pots[0, dst_y, :] = jnp.zeros((window, nz), jnp.float32)

    locals_ = [
        pltpu.make_async_copy(orb.at[0, :, src_y, :], orbs.at[t, :planes, dst_y, :], loc.at[0]),
        pltpu.make_async_copy(tri.at[:, :, src_y, :], wide.at[:, :planes, dst_y, :], loc.at[1]),
        pltpu.make_async_copy(pot.at[:, src_y, :], pots.at[1 : planes + 1, dst_y, :], loc.at[2]),
        pltpu.make_async_copy(par, pars.at[t], loc.at[3]),
        pltpu.make_async_copy(par, freqs.at[f], loc.at[4]),
    ]
    for copy in locals_:
        copy.start()

    def device(k):
        dt, ds, df = k // (ns * nf), (k // nf) % ns, k % nf
        return lax.rem(t + dt, nt), lax.rem(s + ds, ns), lax.rem(f + df, nf)

    count = nt * ns * nf
    barrier = pltpu.get_barrier_semaphore()

    if count <= 64:
        for k in range(1, count):
            pt, ps, pf = device(k)
            pl.semaphore_signal(barrier, inc=1, device_id={"trial": pt, "slab": ps, "freq": pf}, device_id_type=MESH)
    else:

        @pl.loop(1, count)
        def _(k):
            pt, ps, pf = device(k)
            pl.semaphore_signal(barrier, inc=1, device_id={"trial": pt, "slab": ps, "freq": pf}, device_id_type=MESH)

    pl.semaphore_wait(barrier, count - 1)

    def remote(src, dst, send, recv, **where):
        return pltpu.make_async_remote_copy(
            src_ref=src, dst_ref=dst, send_sem=send, recv_sem=recv, device_id=where, device_id_type=MESH
        )

    below, above = jnp.maximum(s - 1, 0), jnp.minimum(s + 1, ns - 1)
    down = [
        remote(orb.at[0, :REACH, src_y, :], orbs.at[t, planes:, dst_y, :], near_s.at[0], near_r.at[0], slab=below),
        remote(tri.at[:, :REACH, src_y, :], wide.at[:, planes:, dst_y, :], near_s.at[1], near_r.at[1], slab=below),
        remote(pot.at[:REACH, src_y, :], pots.at[planes + 1 :, dst_y, :], near_s.at[2], near_r.at[2], slab=below),
    ]
    lift = remote(pot.at[planes - 1, src_y, :], pots.at[0, dst_y, :], near_s.at[3], near_r.at[3], slab=above)

    par_copies = []
    for j in range(1, nt):
        par_copies.append(remote(par, pars.at[t], par_s.at[j], par_r.at[j], trial=lax.rem(t + j, nt)))
    for j in range(1, nf):
        par_copies.append(remote(par, freqs.at[f], frq_s.at[j], frq_r.at[j], freq=lax.rem(f + j, nf)))

    chips = nt // 2
    z = t // 2
    after, before = lax.rem(t + 2, nt), lax.rem(t + nt - 2, nt)
    parts = (slice(0, planes), slice(planes, planes + REACH))

    def block(slot, part):
        return orbs.at[slot, parts[part], dst_y, :]

    def at(hops):
        return lax.rem(t + 2 * hops + nt, nt)

    def from_below(j, part, source=None):
        here = block(at(1 - j), part)
        return remote(here if source is None else source, here, up_s.at[j, part], up_r.at[j, part], trial=after)

    def from_above(j, part, source=None):
        here = block(at(j - 1), part)
        return remote(here if source is None else source, here, dn_s.at[j, part], dn_r.at[j, part], trial=before)

    def handed(hops, part, source=None):
        here = block(at(hops), part)
        index = hops + chips
        return remote(here if source is None else source, here, pass_s.at[index, part], pass_r.at[index, part], trial=mate)

    can_rise, can_sink = z + 1 < chips, z >= 1

    def when(condition, action):
        pl.when(condition)(action)

    when(s > 0, lambda: down[0].start())
    for copy in par_copies:
        copy.start()
    own = orb.at[0, :, src_y, :]
    when(can_rise, lambda: from_below(1, 0, own).start())
    when(can_sink, lambda: from_above(1, 0, own).start())
    handed(0, 0, own).start()

    @pl.when(s > 0)
    def _():
        down[2].start()
        down[1].start()

    when(s < ns - 1, lambda: lift.start())
    when(s < ns - 1, lambda: down[0].wait_recv())
    when(can_rise, lambda: from_below(1, 1).start())
    when(can_sink, lambda: from_above(1, 1).start())
    handed(0, 1).start()

    tri_copies = []
    span = half // piece
    for j in range(1, nt):
        peer = lax.rem(t + j, nt)
        y0 = pl.multiple_of(f * half + lax.rem(peer, span) * piece, 8)
        part = tri.at[:, peer // span, pl.ds(y0, piece), :]
        tri_copies.append(remote(part, tri_in.at[t], tri_s.at[j], tri_r.at[j], trial=peer))
    y0 = pl.multiple_of(f * half + lax.rem(t, span) * piece, 8)
    own_tri = pltpu.make_async_copy(tri.at[:, t // span, pl.ds(y0, piece), :], tri_in.at[t], loc.at[5])
    own_tri.start()

    for j in range(1, chips):
        if j == chips - 1:
            for copy in tri_copies:
                copy.start()
        for part in range(2):

            @pl.when(z >= j)
            def _():
                from_below(j, part).wait_recv()
                if j + 1 < chips:
                    when(can_rise, lambda: from_below(j + 1, part).start())
                handed(-j, part).start()

            @pl.when(z + j < chips)
            def _():
                from_above(j, part).wait_recv()
                if j + 1 < chips:
                    when(can_sink, lambda: from_above(j + 1, part).start())
                handed(j, part).start()

    for copy in locals_:
        copy.wait()
    for copy in par_copies:
        copy.wait_recv()

    inverse = 1.0 / 4.5
    hop = -0.5 / 4.5
    for i in range(norb):
        energy = pars[i, 0:1, :]
        terms = [0.0, 0.0, 0.0, 0.0]
        for w in range(nf):
            mu = (energy + freqs[w, 5:6, :]) * inverse
            c0, c1, c2, c3 = (freqs[w, 1 + n : 2 + n, :] for n in range(4))
            b0, b1, b2, b3 = c0 - c2, c1 - 3.0 * c3, 2.0 * c2, 4.0 * c3
            terms[0] += b0 - mu * (b1 - mu * (b2 - mu * b3))
            terms[1] += b1 - mu * (2.0 * b2 - 3.0 * mu * b3)
            terms[2] += b2 - 3.0 * mu * b3
            terms[3] += b3
        for n in range(4):
            weights[n, i] = jnp.broadcast_to(terms[n], weights.shape[2:])

    when(s < ns - 1, lambda: down[2].wait_recv())
    when(s > 0, lambda: lift.wait_recv())
    for part in range(2):
        handed(0, part).wait_recv()
        for j in range(1, chips):
            when(z >= j, lambda: handed(-j, part).wait_recv())
            when(z + j < chips, lambda: handed(j, part).wait_recv())

    mid = slice(8, 8 + half)
    lane = lax.broadcasted_iota(jnp.int32, (half, nz), 1)
    row = lax.broadcasted_iota(jnp.int32, (half, nz), 0) + f * half

    def links(position, size):
        return (position >= 1).astype(jnp.float32) + (position + 1 < size).astype(jnp.float32)

    def one_plane(x, carry):
        xg = s * planes + x
        column = jnp.zeros((half, nz), jnp.int32) + xg
        for dz in range(-REACH, REACH + 1):
            group = [(n, off) for n, off in enumerate(OFFSETS) if off[2] == dz]
            if not group:
                continue
            depth = lane - dz
            inside = ((depth >= 0) & (depth < nz)).astype(jnp.float32)
            deepest = max(sum(map(abs, off)) for _, off in group)
            least = min(sum(map(abs, off)) for _, off in group)

            def prepare(i, carry):
                centre = rolled(orbs[i, x, mid, :], dz) * inside
                for n in range(least, 4):
                    scaled[n, i] = weights[n, i, 0:1, :] * centre
                return carry

            lax.fori_loop(0, norb, prepare, 0, unroll=True)

            def local(a, b, c):
                return rolled(pots[1 + x + a, 8 + b : 8 + b + half, :], dz - c) * inverse

            for index, (dx, dy, _) in group:
                steps = abs(dx) + abs(dy) + abs(dz)
                sums = {n: 0.0 for n in range(steps, 4)}
                for i in range(norb):
                    there = orbs[i, x + dx, 8 + dy : 8 + dy + half, :]
                    for n in sums:
                        sums[n] = sums[n] + scaled[n, i] * there
                if steps == 3:
                    kind = tuple(sorted(map(abs, (dx, dy, dz))))
                    coef = (PATHS[kind] * hop**3) * sums[3]
                elif steps == 2:
                    here, end = local(0, 0, 0), local(dx, dy, dz)
                    corners = [c for c in ((dx, 0, 0), (0, dy, 0), (0, 0, dz)) if c != (0, 0, 0)]
                    if len(corners) == 1:
                        middle = local(dx // 2, dy // 2, dz // 2)
                        coef = hop**2 * (sums[2] + (here + middle + end) * sums[3])
                    else:
                        middle = local(*corners[0]) + local(*corners[1])
                        coef = hop**2 * (2.0 * sums[2] + (2.0 * (here + end) + middle) * sums[3])
                elif steps == 1:
                    here, end = local(0, 0, 0), local(dx, dy, dz)
                    place = (column, row, depth)
                    size = (planes * ns, ny, nz)
                    move = (dx, dy, dz)
                    side, along = 0.0, 0.0
                    for axis in range(3):
                        if move[axis]:
                            along = links(place[axis], size[axis]) + links(place[axis] + move[axis], size[axis])
                        else:
                            side = side + links(place[axis], size[axis])
                    walks = along + 3.0 * side - 1.0
                    cubic = here * here + here * end + end * end + hop**2 * walks
                    coef = hop * (sums[1] + (here + end) * sums[2] + cubic * sums[3])
                else:
                    here = local(0, 0, 0)
                    degree = links(column, planes * ns) + links(row, ny) + links(lane, nz)
                    near = local(1, 0, 0) + local(-1, 0, 0) + local(0, 1, 0) + local(0, -1, 0)
                    near = near + jnp.where(lane + 1 < nz, local(0, 0, 1), 0.0)
                    near = near + jnp.where(lane >= 1, local(0, 0, -1), 0.0)
                    square = here * here + hop**2 * degree
                    cube = here * (here * here + 2.0 * hop**2 * degree) + hop**2 * near
                    coef = 0.5 * (sums[0] + here * sums[1] + square * sums[2] + cube * sums[3])
                coefs[x, index] = coef
        return carry

    lax.fori_loop(0, planes, one_plane, 0)
    when(s < ns - 1, lambda: down[1].wait_recv())

    def rho_copy(peer):
        return remote(dens.at[peer], rho_in.at[t], rho_s.at[peer], rho_r.at[t], trial=peer)

    def send(x):
        for h in range(span):
            peer = x * span + h
            when(peer != t, lambda: rho_copy(peer).start())

    def plane_at(step):
        return lax.rem(t // span + 1 + step, planes)

    def densities(step, carry):
        x = plane_at(step)

        def one_trial(k, carry):
            density = 0.0
            for dz in range(-REACH, REACH + 1):
                group = [(n, off) for n, off in enumerate(OFFSETS) if off[2] == dz]
                if not group:
                    continue
                part = 0.0
                for index, (dx, dy, _) in group:
                    part = part + coefs[x, index] * wide[k, x + dx, 8 + dy : 8 + dy + half, :]
                density = density + rolled(part, -dz)
            for h in range(span):
                dens[x * span + h, k] = density[h * piece : (h + 1) * piece]
            return carry

        lax.fori_loop(0, per, one_trial, 0)
        when(step > 0, lambda: send(plane_at(step - 1)))
        return carry

    lax.fori_loop(0, planes, densities, 0)
    send(plane_at(planes - 1))

    rho_in[t] = dens[t]
    own_tri.wait()
    for copy in tri_copies:
        copy.wait_recv()
    for j in range(1, nt):
        source = lax.rem(t + j, nt)
        remote(dens.at[source], rho_in.at[source], rho_s.at[source], rho_r.at[source], trial=source).wait_recv()

    contract = (((1,), (1,)), ((), ()))

    def dot(a, b):
        return lax.dot_general(a, b, contract, precision=HIGH, preferred_element_type=jnp.float32)

    gram = jnp.zeros((total, total), jnp.float32)
    for r in range(piece):
        left = tri_in[:, :, r, :].reshape(total, nz)
        right = rho_in[:, :, r, :].reshape(total, nz)
        gram = gram + dot(left, right) + dot(right, left)
    pick = (order[...] == lax.broadcasted_iota(jnp.int32, (total, total), 1)).astype(jnp.float32)
    half_way = jnp.dot(pick, gram, precision=HIGH, preferred_element_type=jnp.float32)
    factor = 1.0 / jnp.sqrt(jnp.float32(planes * ns * ny * nz * norb))
    final = dot(half_way, pick) * factor
    owned = total // (nt * ns)
    for r in range(nt * ns):
        rows_out[r] = final[r * owned : (r + 1) * owned]

    def me():
        return (t * ns + s) * nf + f

    def row_copy(k):
        pt, ps, pf = device(k)
        return remote(
            rows_out.at[pt * ns + ps], rows_in.at[me()], row_s.at[k], row_r.at[k], trial=pt, slab=ps, freq=pf
        )

    def each(action):
        if count <= 64:
            for k in range(1, count):
                action(k)
        else:
            pl.loop(1, count)(action)

    each(lambda k: row_copy(k).start())
    rows_in[me()] = rows_out[t * ns + s]
    each(lambda k: row_copy(k).wait())
    out[...] = jnp.sum(rows_in[...], axis=0)

    for j in range(1, nt):
        rho_copy(lax.rem(t + j, nt)).wait_send()
    for copy in par_copies + tri_copies:
        copy.wait_send()
    for part in range(2):
        first = own if part == 0 else None
        when(can_rise, lambda: from_below(1, part, first).wait_send())
        when(can_sink, lambda: from_above(1, part, first).wait_send())
        handed(0, part, first).wait_send()
        for j in range(1, chips):
            if j + 1 < chips:
                when(can_rise & (z >= j), lambda: from_below(j + 1, part).wait_send())
                when(can_sink & (z + j < chips), lambda: from_above(j + 1, part).wait_send())
            when(z >= j, lambda: handed(-j, part).wait_send())
            when(z + j < chips, lambda: handed(j, part).wait_send())

    @pl.when(s > 0)
    def _():
        for copy in down:
            copy.wait_send()

    when(s < ns - 1, lambda: lift.wait_send())


def local(sizes, orbitals, energies, potential, trials, cheb, shifts, column_order):
    nt, ns, nf = sizes
    per, planes, ny, nz = trials.shape
    norb = orbitals.shape[0] * nt
    half = ny // nf
    full = half + 16
    total = nt * per
    piece = planes * half // nt
    owned = total // (nt * ns)
    count = nt * ns * nf
    chips = nt // 2
    column = jnp.concatenate([energies, cheb[0], shifts, jnp.zeros((2,), jnp.float32)])
    par = jnp.broadcast_to(column[:, None], (8, 128))
    f32 = jnp.float32
    dma = pltpu.SemaphoreType.DMA
    anywhere = pl.BlockSpec(memory_space=pltpu.HBM)
    vmem = pl.BlockSpec(memory_space=pltpu.VMEM)
    return pl.pallas_call(
        functools.partial(kernel, sizes),
        out_shape=jax.ShapeDtypeStruct((owned, total), f32),
        in_specs=[anywhere, vmem, anywhere, anywhere, vmem],
        out_specs=vmem,
        scratch_shapes=[
            pltpu.VMEM((norb, planes + REACH, full, nz), f32),
            pltpu.VMEM((per, planes + REACH, full, nz), f32),
            pltpu.VMEM((planes + REACH + 1, full, nz), f32),
            pltpu.VMEM((nt, 8, 128), f32),
            pltpu.VMEM((nf, 8, 128), f32),
            pltpu.VMEM((4, norb, half, nz), f32),
            pltpu.VMEM((4, norb, 8, nz), f32),
            pltpu.VMEM((planes, len(OFFSETS), half, nz), f32),
            pltpu.VMEM((nt, per, piece, nz), f32),
            pltpu.VMEM((nt, per, piece, nz), f32),
            pltpu.VMEM((nt, per, piece, nz), f32),
            pltpu.VMEM((nt * ns, owned, total), f32),
            pltpu.VMEM((count, owned, total), f32),
            dma((4,)), dma((4,)), dma((chips, 2)), dma((chips, 2)), dma((chips, 2)), dma((chips, 2)),
            dma((2 * chips, 2)), dma((2 * chips, 2)), dma((nt,)), dma((nt,)), dma((nf,)), dma((nf,)), dma((nt,)), dma((nt,)), dma((nt,)), dma((nt,)), dma((count,)), dma((count,)),
            dma((6,)),
        ],
        compiler_params=pltpu.CompilerParams(
            collective_id=0, has_side_effects=True, vmem_limit_bytes=48 * 1024 * 1024
        ),
    )(orbitals, par, potential, trials, column_order[:, None])


def solution(mesh):
    sizes = tuple(mesh.shape[name] for name in ("trial", "slab", "freq"))
    in_specs = (
        P("trial", "slab", None, None),
        P("trial"),
        P("slab", None, None),
        P("trial", "slab", None, None),
        P("freq", None),
        P("freq"),
        P(),
    )
    out_specs = P(("trial", "slab"), None)
    return jax.shard_map(
        functools.partial(local, sizes), mesh=mesh, in_specs=in_specs, out_specs=out_specs, check_vma=False
    )
```

```python
import functools

import jax
import jax.numpy as jnp
from jax import lax
from jax.experimental import pallas as pl
from jax.experimental.pallas import tpu as pltpu
from jax.sharding import PartitionSpec as P

REACH = 3
MESH = pl.DeviceIdType.MESH
HIGH = lax.Precision.HIGHEST

OFFSETS = [
    (dx, dy, dz)
    for dz in range(-REACH, REACH + 1)
    for dx in range(REACH + 1)
    for dy in range(-REACH, REACH + 1)
    if abs(dx) + abs(dy) + abs(dz) <= REACH and (dx, dy, dz) >= (0, 0, 0)
]
PATHS = {(1, 1, 1): 6.0, (0, 1, 2): 3.0, (0, 0, 3): 1.0}


def rolled(value, shift):
    shift = shift % value.shape[1]
    return value if shift == 0 else pltpu.roll(value, shift, 1)


def kernel(
    sizes, orb, par, pot, tri, order, out,
    orbs, wide, pots, pars, freqs, scaled, weights, coefs, dens, rho_in, tri_in, rows_out, rows_in,
    near_s, near_r, up_s, up_r, dn_s, dn_r, pass_s, pass_r, par_s, par_r, frq_s, frq_r,
    tri_s, tri_r, rho_s, rho_r, row_s, row_r, loc, picks,
):
    nt, ns, nf = sizes
    per, planes, ny, nz = tri.shape
    norb = orbs.shape[0]
    half = ny // nf
    window = half + 8
    total = nt * per
    piece = planes * half // nt
    t, s, f = lax.axis_index("trial"), lax.axis_index("slab"), lax.axis_index("freq")
    mate = t + 1 - 2 * lax.rem(t, 2)
    src_y = pl.ds(pl.multiple_of(f * (half - 8), 8), window)
    dst_y = pl.ds(pl.multiple_of(8 - 8 * f, 8), window)
    edge_y = pl.ds(pl.multiple_of(f * window, 8), 8)
    last = s == ns - 1

    orbs[:, :, edge_y, :] = jnp.zeros((norb, planes + REACH, 8, nz), jnp.float32)
    wide[:, :, edge_y, :] = jnp.zeros((per, planes + REACH, 8, nz), jnp.float32)
    pots[:, edge_y, :] = jnp.zeros((planes + REACH + 1, 8, nz), jnp.float32)

    @pl.when(last)
    def _():
        orbs[t, planes:, dst_y, :] = jnp.zeros((REACH, window, nz), jnp.float32)
        wide[:, planes:, dst_y, :] = jnp.zeros((per, REACH, window, nz), jnp.float32)
        pots[planes + 1 :, dst_y, :] = jnp.zeros((REACH, window, nz), jnp.float32)

    @pl.when(s == 0)
    def _():
        pots[0, dst_y, :] = jnp.zeros((window, nz), jnp.float32)

    locals_ = [
        pltpu.make_async_copy(orb.at[0, :, src_y, :], orbs.at[t, :planes, dst_y, :], loc.at[0]),
        pltpu.make_async_copy(tri.at[:, :, src_y, :], wide.at[:, :planes, dst_y, :], loc.at[1]),
        pltpu.make_async_copy(pot.at[:, src_y, :], pots.at[1 : planes + 1, dst_y, :], loc.at[2]),
        pltpu.make_async_copy(par, pars.at[t], loc.at[3]),
        pltpu.make_async_copy(par, freqs.at[f], loc.at[4]),
        pltpu.make_async_copy(order, picks, loc.at[6]),
    ]
    for copy in locals_:
        copy.start()

    def device(k):
        dt, ds, df = k // (ns * nf), (k // nf) % ns, k % nf
        return lax.rem(t + dt, nt), lax.rem(s + ds, ns), lax.rem(f + df, nf)

    count = nt * ns * nf
    barrier = pltpu.get_barrier_semaphore()

    if count <= 64:
        for k in range(1, count):
            pt, ps, pf = device(k)
            pl.semaphore_signal(barrier, inc=1, device_id={"trial": pt, "slab": ps, "freq": pf}, device_id_type=MESH)
    else:

        @pl.loop(1, count)
        def _(k):
            pt, ps, pf = device(k)
            pl.semaphore_signal(barrier, inc=1, device_id={"trial": pt, "slab": ps, "freq": pf}, device_id_type=MESH)

    pl.semaphore_wait(barrier, count - 1)

    def remote(src, dst, send, recv, **where):
        return pltpu.make_async_remote_copy(
            src_ref=src, dst_ref=dst, send_sem=send, recv_sem=recv, device_id=where, device_id_type=MESH
        )

    below, above = jnp.maximum(s - 1, 0), jnp.minimum(s + 1, ns - 1)
    down = [
        remote(orb.at[0, :REACH, src_y, :], orbs.at[t, planes:, dst_y, :], near_s.at[0], near_r.at[0], slab=below),
        remote(tri.at[:, :REACH, src_y, :], wide.at[:, planes:, dst_y, :], near_s.at[1], near_r.at[1], slab=below),
        remote(pot.at[:REACH, src_y, :], pots.at[planes + 1 :, dst_y, :], near_s.at[2], near_r.at[2], slab=below),
    ]
    lift = remote(pot.at[planes - 1, src_y, :], pots.at[0, dst_y, :], near_s.at[3], near_r.at[3], slab=above)

    par_copies = []
    for j in range(1, nt):
        par_copies.append(remote(par, pars.at[t], par_s.at[j], par_r.at[j], trial=lax.rem(t + j, nt)))
    for j in range(1, nf):
        par_copies.append(remote(par, freqs.at[f], frq_s.at[j], frq_r.at[j], freq=lax.rem(f + j, nf)))

    chips = nt // 2
    z = t // 2
    after, before = lax.rem(t + 2, nt), lax.rem(t + nt - 2, nt)
    parts = (slice(0, planes), slice(planes, planes + REACH))

    def block(slot, part):
        return orbs.at[slot, parts[part], dst_y, :]

    def at(hops):
        return lax.rem(t + 2 * hops + nt, nt)

    def from_below(j, part, source=None):
        here = block(at(1 - j), part)
        return remote(here if source is None else source, here, up_s.at[j, part], up_r.at[j, part], trial=after)

    def from_above(j, part, source=None):
        here = block(at(j - 1), part)
        return remote(here if source is None else source, here, dn_s.at[j, part], dn_r.at[j, part], trial=before)

    def handed(hops, part, source=None):
        here = block(at(hops), part)
        index = hops + chips
        return remote(here if source is None else source, here, pass_s.at[index, part], pass_r.at[index, part], trial=mate)

    can_rise, can_sink = z + 1 < chips, z >= 1

    def when(condition, action):
        pl.when(condition)(action)

    when(s > 0, lambda: down[0].start())
    for copy in par_copies:
        copy.start()
    own = orb.at[0, :, src_y, :]
    when(can_rise, lambda: from_below(1, 0, own).start())
    when(can_sink, lambda: from_above(1, 0, own).start())
    handed(0, 0, own).start()

    @pl.when(s > 0)
    def _():
        down[2].start()
        down[1].start()

    when(s < ns - 1, lambda: lift.start())
    when(s < ns - 1, lambda: down[0].wait_recv())
    when(can_rise, lambda: from_below(1, 1).start())
    when(can_sink, lambda: from_above(1, 1).start())
    handed(0, 1).start()

    tri_copies = []
    span = half // piece
    for j in range(1, nt):
        peer = lax.rem(t + j, nt)
        y0 = pl.multiple_of(f * half + lax.rem(peer, span) * piece, 8)
        part = tri.at[:, peer // span, pl.ds(y0, piece), :]
        tri_copies.append(remote(part, tri_in.at[t], tri_s.at[j], tri_r.at[j], trial=peer))
    y0 = pl.multiple_of(f * half + lax.rem(t, span) * piece, 8)
    own_tri = pltpu.make_async_copy(tri.at[:, t // span, pl.ds(y0, piece), :], tri_in.at[t], loc.at[5])
    own_tri.start()

    for j in range(1, chips):
        if j == chips - 1:
            for copy in tri_copies:
                copy.start()
        for part in range(2):

            @pl.when(z >= j)
            def _():
                from_below(j, part).wait_recv()
                if j + 1 < chips:
                    when(can_rise, lambda: from_below(j + 1, part).start())
                handed(-j, part).start()

            @pl.when(z + j < chips)
            def _():
                from_above(j, part).wait_recv()
                if j + 1 < chips:
                    when(can_sink, lambda: from_above(j + 1, part).start())
                handed(j, part).start()

    for copy in locals_:
        copy.wait()
    for copy in par_copies:
        copy.wait_recv()

    inverse = 1.0 / 4.5
    hop = -0.5 / 4.5
    for i in range(norb):
        energy = pars[i, 0:1, :]
        terms = [0.0, 0.0, 0.0, 0.0]
        for w in range(nf):
            mu = (energy + freqs[w, 5:6, :]) * inverse
            c0, c1, c2, c3 = (freqs[w, 1 + n : 2 + n, :] for n in range(4))
            b0, b1, b2, b3 = c0 - c2, c1 - 3.0 * c3, 2.0 * c2, 4.0 * c3
            terms[0] += b0 - mu * (b1 - mu * (b2 - mu * b3))
            terms[1] += b1 - mu * (2.0 * b2 - 3.0 * mu * b3)
            terms[2] += b2 - 3.0 * mu * b3
            terms[3] += b3
        for n in range(4):
            weights[n, i] = jnp.broadcast_to(terms[n], weights.shape[2:])

    when(s < ns - 1, lambda: down[2].wait_recv())
    when(s > 0, lambda: lift.wait_recv())
    for part in range(2):
        handed(0, part).wait_recv()
        for j in range(1, chips):
            when(z >= j, lambda: handed(-j, part).wait_recv())
            when(z + j < chips, lambda: handed(j, part).wait_recv())

    mid = slice(8, 8 + half)
    lane = lax.broadcasted_iota(jnp.int32, (half, nz), 1)
    row = lax.broadcasted_iota(jnp.int32, (half, nz), 0) + f * half

    def links(position, size):
        return (position >= 1).astype(jnp.float32) + (position + 1 < size).astype(jnp.float32)

    def one_plane(x, carry):
        xg = s * planes + x
        column = jnp.zeros((half, nz), jnp.int32) + xg
        for dz in range(-REACH, REACH + 1):
            group = [(n, off) for n, off in enumerate(OFFSETS) if off[2] == dz]
            if not group:
                continue
            depth = lane - dz
            inside = ((depth >= 0) & (depth < nz)).astype(jnp.float32)
            deepest = max(sum(map(abs, off)) for _, off in group)
            least = min(sum(map(abs, off)) for _, off in group)

            def prepare(i, carry):
                centre = rolled(orbs[i, x, mid, :], dz) * inside
                for n in range(least, 4):
                    scaled[n, i] = weights[n, i, 0:1, :] * centre
                return carry

            lax.fori_loop(0, norb, prepare, 0, unroll=True)

            def local(a, b, c):
                return rolled(pots[1 + x + a, 8 + b : 8 + b + half, :], dz - c) * inverse

            for index, (dx, dy, _) in group:
                steps = abs(dx) + abs(dy) + abs(dz)
                sums = {n: 0.0 for n in range(steps, 4)}
                for i in range(norb):
                    there = orbs[i, x + dx, 8 + dy : 8 + dy + half, :]
                    for n in sums:
                        sums[n] = sums[n] + scaled[n, i] * there
                if steps == 3:
                    kind = tuple(sorted(map(abs, (dx, dy, dz))))
                    coef = (PATHS[kind] * hop**3) * sums[3]
                elif steps == 2:
                    here, end = local(0, 0, 0), local(dx, dy, dz)
                    corners = [c for c in ((dx, 0, 0), (0, dy, 0), (0, 0, dz)) if c != (0, 0, 0)]
                    if len(corners) == 1:
                        middle = local(dx // 2, dy // 2, dz // 2)
                        coef = hop**2 * (sums[2] + (here + middle + end) * sums[3])
                    else:
                        middle = local(*corners[0]) + local(*corners[1])
                        coef = hop**2 * (2.0 * sums[2] + (2.0 * (here + end) + middle) * sums[3])
                elif steps == 1:
                    here, end = local(0, 0, 0), local(dx, dy, dz)
                    place = (column, row, depth)
                    size = (planes * ns, ny, nz)
                    move = (dx, dy, dz)
                    side, along = 0.0, 0.0
                    for axis in range(3):
                        if move[axis]:
                            along = links(place[axis], size[axis]) + links(place[axis] + move[axis], size[axis])
                        else:
                            side = side + links(place[axis], size[axis])
                    walks = along + 3.0 * side - 1.0
                    cubic = here * here + here * end + end * end + hop**2 * walks
                    coef = hop * (sums[1] + (here + end) * sums[2] + cubic * sums[3])
                else:
                    here = local(0, 0, 0)
                    degree = links(column, planes * ns) + links(row, ny) + links(lane, nz)
                    near = local(1, 0, 0) + local(-1, 0, 0) + local(0, 1, 0) + local(0, -1, 0)
                    near = near + jnp.where(lane + 1 < nz, local(0, 0, 1), 0.0)
                    near = near + jnp.where(lane >= 1, local(0, 0, -1), 0.0)
                    square = here * here + hop**2 * degree
                    cube = here * (here * here + 2.0 * hop**2 * degree) + hop**2 * near
                    coef = 0.5 * (sums[0] + here * sums[1] + square * sums[2] + cube * sums[3])
                coefs[x, index] = coef
        return carry

    lax.fori_loop(0, planes, one_plane, 0)
    when(s < ns - 1, lambda: down[1].wait_recv())

    def rho_copy(peer):
        return remote(dens.at[peer], rho_in.at[t], rho_s.at[peer], rho_r.at[t], trial=peer)

    def send(x):
        for h in range(span):
            peer = x * span + h
            when(peer != t, lambda: rho_copy(peer).start())

    def plane_at(step):
        return lax.rem(t // span + 1 + step, planes)

    def densities(step, carry):
        x = plane_at(step)

        def one_trial(k, carry):
            density = 0.0
            for dz in range(-REACH, REACH + 1):
                group = [(n, off) for n, off in enumerate(OFFSETS) if off[2] == dz]
                if not group:
                    continue
                part = 0.0
                for index, (dx, dy, _) in group:
                    part = part + coefs[x, index] * wide[k, x + dx, 8 + dy : 8 + dy + half, :]
                density = density + rolled(part, -dz)
            for h in range(span):
                dens[x * span + h, k] = density[h * piece : (h + 1) * piece]
            return carry

        lax.fori_loop(0, per, one_trial, 0)
        when(step > 0, lambda: send(plane_at(step - 1)))
        return carry

    lax.fori_loop(0, planes, densities, 0)
    send(plane_at(planes - 1))

    rho_in[t] = dens[t]
    own_tri.wait()
    for copy in tri_copies:
        copy.wait_recv()
    for j in range(1, nt):
        source = lax.rem(t + j, nt)
        remote(dens.at[source], rho_in.at[source], rho_s.at[source], rho_r.at[source], trial=source).wait_recv()

    contract = (((1,), (1,)), ((), ()))

    def dot(a, b):
        return lax.dot_general(a, b, contract, precision=HIGH, preferred_element_type=jnp.float32)

    gram = jnp.zeros((total, total), jnp.float32)
    for r in range(piece):
        left = tri_in[:, :, r, :].reshape(total, nz)
        right = rho_in[:, :, r, :].reshape(total, nz)
        gram = gram + dot(left, right) + dot(right, left)
    pick = (picks[...] == lax.broadcasted_iota(jnp.int32, (total, total), 0)).astype(jnp.float32)
    half_way = lax.dot_general(
        pick, gram, (((0,), (0,)), ((), ())), precision=HIGH, preferred_element_type=jnp.float32
    )
    factor = 1.0 / jnp.sqrt(jnp.float32(planes * ns * ny * nz * norb))
    final = jnp.dot(half_way, pick, precision=HIGH, preferred_element_type=jnp.float32) * factor
    owned = total // (nt * ns)
    for r in range(nt * ns):
        rows_out[r] = final[r * owned : (r + 1) * owned]

    def me():
        return (t * ns + s) * nf + f

    def row_copy(k):
        pt, ps, pf = device(k)
        return remote(
            rows_out.at[pt * ns + ps], rows_in.at[me()], row_s.at[k], row_r.at[k], trial=pt, slab=ps, freq=pf
        )

    def each(action):
        if count <= 64:
            for k in range(1, count):
                action(k)
        else:
            pl.loop(1, count)(action)

    each(lambda k: row_copy(k).start())
    rows_in[me()] = rows_out[t * ns + s]
    each(lambda k: row_copy(k).wait())
    out[...] = jnp.sum(rows_in[...], axis=0)

    for j in range(1, nt):
        rho_copy(lax.rem(t + j, nt)).wait_send()
    for copy in par_copies + tri_copies:
        copy.wait_send()
    for part in range(2):
        first = own if part == 0 else None
        when(can_rise, lambda: from_below(1, part, first).wait_send())
        when(can_sink, lambda: from_above(1, part, first).wait_send())
        handed(0, part, first).wait_send()
        for j in range(1, chips):
            if j + 1 < chips:
                when(can_rise & (z >= j), lambda: from_below(j + 1, part).wait_send())
                when(can_sink & (z + j < chips), lambda: from_above(j + 1, part).wait_send())
            when(z >= j, lambda: handed(-j, part).wait_send())
            when(z + j < chips, lambda: handed(j, part).wait_send())

    @pl.when(s > 0)
    def _():
        for copy in down:
            copy.wait_send()

    when(s < ns - 1, lambda: lift.wait_send())


def local(sizes, orbitals, energies, potential, trials, cheb, shifts, column_order):
    nt, ns, nf = sizes
    per, planes, ny, nz = trials.shape
    norb = orbitals.shape[0] * nt
    half = ny // nf
    full = half + 16
    total = nt * per
    piece = planes * half // nt
    owned = total // (nt * ns)
    count = nt * ns * nf
    chips = nt // 2
    column = jnp.concatenate([energies, cheb[0], shifts, jnp.zeros((2,), jnp.float32)])
    par = jnp.broadcast_to(column[:, None], (8, 128))
    f32 = jnp.float32
    dma = pltpu.SemaphoreType.DMA
    anywhere = pl.BlockSpec(memory_space=pltpu.HBM)
    vmem = pl.BlockSpec(memory_space=pltpu.VMEM)
    return pl.pallas_call(
        functools.partial(kernel, sizes),
        out_shape=jax.ShapeDtypeStruct((owned, total), f32),
        in_specs=[anywhere, vmem, anywhere, anywhere, anywhere],
        out_specs=vmem,
        scratch_shapes=[
            pltpu.VMEM((norb, planes + REACH, full, nz), f32),
            pltpu.VMEM((per, planes + REACH, full, nz), f32),
            pltpu.VMEM((planes + REACH + 1, full, nz), f32),
            pltpu.VMEM((nt, 8, 128), f32),
            pltpu.VMEM((nf, 8, 128), f32),
            pltpu.VMEM((4, norb, half, nz), f32),
            pltpu.VMEM((4, norb, 8, nz), f32),
            pltpu.VMEM((planes, len(OFFSETS), half, nz), f32),
            pltpu.VMEM((nt, per, piece, nz), f32),
            pltpu.VMEM((nt, per, piece, nz), f32),
            pltpu.VMEM((nt, per, piece, nz), f32),
            pltpu.VMEM((nt * ns, owned, total), f32),
            pltpu.VMEM((count, owned, total), f32),
            dma((4,)), dma((4,)), dma((chips, 2)), dma((chips, 2)), dma((chips, 2)), dma((chips, 2)),
            dma((2 * chips, 2)), dma((2 * chips, 2)), dma((nt,)), dma((nt,)), dma((nf,)), dma((nf,)), dma((nt,)), dma((nt,)), dma((nt,)), dma((nt,)), dma((count,)), dma((count,)),
            dma((7,)),
            pltpu.VMEM((1, total), jnp.int32),
        ],
        compiler_params=pltpu.CompilerParams(
            collective_id=0, has_side_effects=True, vmem_limit_bytes=67043328 - 65536
        ),
    )(orbitals, par, potential, trials, column_order[None])


def solution(mesh):
    sizes = tuple(mesh.shape[name] for name in ("trial", "slab", "freq"))
    in_specs = (
        P("trial", "slab", None, None),
        P("trial"),
        P("slab", None, None),
        P("trial", "slab", None, None),
        P("freq", None),
        P("freq"),
        P(),
    )
    out_specs = P(("trial", "slab"), None)
    return jax.shard_map(
        functools.partial(local, sizes), mesh=mesh, in_specs=in_specs, out_specs=out_specs, check_vma=False
    )
```

```python
import functools

import jax
import jax.numpy as jnp
from jax import lax
from jax.experimental import pallas as pl
from jax.experimental.pallas import tpu as pltpu
from jax.sharding import PartitionSpec as P

REACH = 3
MESH = pl.DeviceIdType.MESH
HIGH = lax.Precision.HIGHEST

OFFSETS = [
    (dx, dy, dz)
    for dz in range(-REACH, REACH + 1)
    for dx in range(REACH + 1)
    for dy in range(-REACH, REACH + 1)
    if abs(dx) + abs(dy) + abs(dz) <= REACH and (dx, dy, dz) >= (0, 0, 0)
]
PATHS = {(1, 1, 1): 6.0, (0, 1, 2): 3.0, (0, 0, 3): 1.0}


def rolled(value, shift):
    shift = shift % value.shape[1]
    return value if shift == 0 else pltpu.roll(value, shift, 1)


def kernel(
    sizes, orb, par, pot, tri, order, out,
    orbs, wide, pots, pars, freqs, scaled, weights, coefs, dens, rho_in, tri_in, rows_out, rows_in,
    near_s, near_r, up_s, up_r, dn_s, dn_r, pass_s, pass_r, par_s, par_r, frq_s, frq_r,
    tri_s, tri_r, rho_s, rho_r, row_s, row_r, loc, picks,
):
    nt, ns, nf = sizes
    per, planes, ny, nz = tri.shape
    norb = orbs.shape[0]
    half = ny // nf
    window = half + 8
    total = nt * per
    piece = planes * half // nt
    t, s, f = lax.axis_index("trial"), lax.axis_index("slab"), lax.axis_index("freq")
    mate = t + 1 - 2 * lax.rem(t, 2)
    src_y = pl.ds(pl.multiple_of(f * (half - 8), 8), window)
    dst_y = pl.ds(pl.multiple_of(8 - 8 * f, 8), window)
    edge_y = pl.ds(pl.multiple_of(f * window, 8), 8)
    last = s == ns - 1

    orbs[:, :, edge_y, :] = jnp.zeros((norb, planes + REACH, 8, nz), jnp.float32)
    wide[:, :, edge_y, :] = jnp.zeros((per, planes + REACH, 8, nz), jnp.float32)
    pots[:, edge_y, :] = jnp.zeros((planes + REACH + 1, 8, nz), jnp.float32)

    @pl.when(last)
    def _():
        orbs[t, planes:, dst_y, :] = jnp.zeros((REACH, window, nz), jnp.float32)
        wide[:, planes:, dst_y, :] = jnp.zeros((per, REACH, window, nz), jnp.float32)
        pots[planes + 1 :, dst_y, :] = jnp.zeros((REACH, window, nz), jnp.float32)

    @pl.when(s == 0)
    def _():
        pots[0, dst_y, :] = jnp.zeros((window, nz), jnp.float32)

    locals_ = [
        pltpu.make_async_copy(orb.at[0, :, src_y, :], orbs.at[t, :planes, dst_y, :], loc.at[0]),
        pltpu.make_async_copy(tri.at[:, :, src_y, :], wide.at[:, :planes, dst_y, :], loc.at[1]),
        pltpu.make_async_copy(pot.at[:, src_y, :], pots.at[1 : planes + 1, dst_y, :], loc.at[2]),
        pltpu.make_async_copy(par, pars.at[t], loc.at[3]),
        pltpu.make_async_copy(par, freqs.at[f], loc.at[4]),
        pltpu.make_async_copy(order, picks, loc.at[6]),
    ]
    for copy in locals_:
        copy.start()

    def device(k):
        dt, ds, df = k // (ns * nf), (k // nf) % ns, k % nf
        return lax.rem(t + dt, nt), lax.rem(s + ds, ns), lax.rem(f + df, nf)

    count = nt * ns * nf
    barrier = pltpu.get_barrier_semaphore()

    if count <= 64:
        for k in range(1, count):
            pt, ps, pf = device(k)
            pl.semaphore_signal(barrier, inc=1, device_id={"trial": pt, "slab": ps, "freq": pf}, device_id_type=MESH)
    else:

        @pl.loop(1, count)
        def _(k):
            pt, ps, pf = device(k)
            pl.semaphore_signal(barrier, inc=1, device_id={"trial": pt, "slab": ps, "freq": pf}, device_id_type=MESH)

    pl.semaphore_wait(barrier, count - 1)

    def remote(src, dst, send, recv, **where):
        return pltpu.make_async_remote_copy(
            src_ref=src, dst_ref=dst, send_sem=send, recv_sem=recv, device_id=where, device_id_type=MESH
        )

    below, above = jnp.maximum(s - 1, 0), jnp.minimum(s + 1, ns - 1)
    down = [
        remote(orb.at[0, :REACH, src_y, :], orbs.at[t, planes:, dst_y, :], near_s.at[0], near_r.at[0], slab=below),
        remote(tri.at[:, :REACH, src_y, :], wide.at[:, planes:, dst_y, :], near_s.at[1], near_r.at[1], slab=below),
        remote(pot.at[:REACH, src_y, :], pots.at[planes + 1 :, dst_y, :], near_s.at[2], near_r.at[2], slab=below),
    ]
    lift = remote(pot.at[planes - 1, src_y, :], pots.at[0, dst_y, :], near_s.at[3], near_r.at[3], slab=above)

    par_copies = []
    for j in range(1, nt):
        par_copies.append(remote(par, pars.at[t], par_s.at[j], par_r.at[j], trial=lax.rem(t + j, nt)))
    for j in range(1, nf):
        par_copies.append(remote(par, freqs.at[f], frq_s.at[j], frq_r.at[j], freq=lax.rem(f + j, nf)))

    chips = nt // 2
    z = t // 2
    after, before = lax.rem(t + 2, nt), lax.rem(t + nt - 2, nt)
    parts = (slice(0, planes), slice(planes, planes + REACH))

    def block(slot, part):
        return orbs.at[slot, parts[part], dst_y, :]

    def at(hops):
        return lax.rem(t + 2 * hops + nt, nt)

    def from_below(j, part, source=None):
        here = block(at(1 - j), part)
        return remote(here if source is None else source, here, up_s.at[j, part], up_r.at[j, part], trial=after)

    def from_above(j, part, source=None):
        here = block(at(j - 1), part)
        return remote(here if source is None else source, here, dn_s.at[j, part], dn_r.at[j, part], trial=before)

    def handed(hops, part, source=None):
        here = block(at(hops), part)
        index = hops + chips
        return remote(here if source is None else source, here, pass_s.at[index, part], pass_r.at[index, part], trial=mate)

    can_rise, can_sink = z + 1 < chips, z >= 1

    def when(condition, action):
        pl.when(condition)(action)

    when(s > 0, lambda: down[0].start())
    own = orb.at[0, :, src_y, :]
    when(can_rise, lambda: from_below(1, 0, own).start())
    when(can_sink, lambda: from_above(1, 0, own).start())
    handed(0, 0, own).start()
    for copy in par_copies:
        copy.start()

    @pl.when(s > 0)
    def _():
        down[2].start()
        down[1].start()

    when(s < ns - 1, lambda: lift.start())
    when(s < ns - 1, lambda: down[0].wait_recv())
    when(can_rise, lambda: from_below(1, 1).start())
    when(can_sink, lambda: from_above(1, 1).start())
    handed(0, 1).start()

    tri_copies = []
    span = half // piece
    for j in range(1, nt):
        peer = lax.rem(t + j, nt)
        y0 = pl.multiple_of(f * half + lax.rem(peer, span) * piece, 8)
        part = tri.at[:, peer // span, pl.ds(y0, piece), :]
        tri_copies.append(remote(part, tri_in.at[t], tri_s.at[j], tri_r.at[j], trial=peer))
    y0 = pl.multiple_of(f * half + lax.rem(t, span) * piece, 8)
    own_tri = pltpu.make_async_copy(tri.at[:, t // span, pl.ds(y0, piece), :], tri_in.at[t], loc.at[5])
    own_tri.start()

    for j in range(1, chips):
        if j == chips - 1:
            for copy in tri_copies:
                copy.start()
        for part in range(2):

            @pl.when(z >= j)
            def _():
                from_below(j, part).wait_recv()
                if j + 1 < chips:
                    when(can_rise, lambda: from_below(j + 1, part).start())
                handed(-j, part).start()

            @pl.when(z + j < chips)
            def _():
                from_above(j, part).wait_recv()
                if j + 1 < chips:
                    when(can_sink, lambda: from_above(j + 1, part).start())
                handed(j, part).start()

    for copy in locals_:
        copy.wait()
    for copy in par_copies:
        copy.wait_recv()

    inverse = 1.0 / 4.5
    hop = -0.5 / 4.5
    for i in range(norb):
        energy = pars[i, 0:1, :]
        terms = [0.0, 0.0, 0.0, 0.0]
        for w in range(nf):
            mu = (energy + freqs[w, 5:6, :]) * inverse
            c0, c1, c2, c3 = (freqs[w, 1 + n : 2 + n, :] for n in range(4))
            b0, b1, b2, b3 = c0 - c2, c1 - 3.0 * c3, 2.0 * c2, 4.0 * c3
            terms[0] += b0 - mu * (b1 - mu * (b2 - mu * b3))
            terms[1] += b1 - mu * (2.0 * b2 - 3.0 * mu * b3)
            terms[2] += b2 - 3.0 * mu * b3
            terms[3] += b3
        for n in range(4):
            weights[n, i] = jnp.broadcast_to(terms[n], weights.shape[2:])

    when(s < ns - 1, lambda: down[2].wait_recv())
    when(s > 0, lambda: lift.wait_recv())
    for part in range(2):
        handed(0, part).wait_recv()
        for j in range(1, chips):
            when(z >= j, lambda: handed(-j, part).wait_recv())
            when(z + j < chips, lambda: handed(j, part).wait_recv())

    mid = slice(8, 8 + half)
    lane = lax.broadcasted_iota(jnp.int32, (half, nz), 1)
    row = lax.broadcasted_iota(jnp.int32, (half, nz), 0) + f * half

    def links(position, size):
        return (position >= 1).astype(jnp.float32) + (position + 1 < size).astype(jnp.float32)

    def one_plane(x, carry):
        xg = s * planes + x
        column = jnp.zeros((half, nz), jnp.int32) + xg
        for dz in range(-REACH, REACH + 1):
            group = [(n, off) for n, off in enumerate(OFFSETS) if off[2] == dz]
            if not group:
                continue
            depth = lane - dz
            inside = ((depth >= 0) & (depth < nz)).astype(jnp.float32)
            deepest = max(sum(map(abs, off)) for _, off in group)
            least = min(sum(map(abs, off)) for _, off in group)

            def prepare(i, carry):
                centre = rolled(orbs[i, x, mid, :], dz) * inside
                for n in range(least, 4):
                    scaled[n, i] = weights[n, i, 0:1, :] * centre
                return carry

            lax.fori_loop(0, norb, prepare, 0, unroll=True)

            def local(a, b, c):
                return rolled(pots[1 + x + a, 8 + b : 8 + b + half, :], dz - c) * inverse

            for index, (dx, dy, _) in group:
                steps = abs(dx) + abs(dy) + abs(dz)
                sums = {n: 0.0 for n in range(steps, 4)}
                for i in range(norb):
                    there = orbs[i, x + dx, 8 + dy : 8 + dy + half, :]
                    for n in sums:
                        sums[n] = sums[n] + scaled[n, i] * there
                if steps == 3:
                    kind = tuple(sorted(map(abs, (dx, dy, dz))))
                    coef = (PATHS[kind] * hop**3) * sums[3]
                elif steps == 2:
                    here, end = local(0, 0, 0), local(dx, dy, dz)
                    corners = [c for c in ((dx, 0, 0), (0, dy, 0), (0, 0, dz)) if c != (0, 0, 0)]
                    if len(corners) == 1:
                        middle = local(dx // 2, dy // 2, dz // 2)
                        coef = hop**2 * (sums[2] + (here + middle + end) * sums[3])
                    else:
                        middle = local(*corners[0]) + local(*corners[1])
                        coef = hop**2 * (2.0 * sums[2] + (2.0 * (here + end) + middle) * sums[3])
                elif steps == 1:
                    here, end = local(0, 0, 0), local(dx, dy, dz)
                    place = (column, row, depth)
                    size = (planes * ns, ny, nz)
                    move = (dx, dy, dz)
                    side, along = 0.0, 0.0
                    for axis in range(3):
                        if move[axis]:
                            along = links(place[axis], size[axis]) + links(place[axis] + move[axis], size[axis])
                        else:
                            side = side + links(place[axis], size[axis])
                    walks = along + 3.0 * side - 1.0
                    cubic = here * here + here * end + end * end + hop**2 * walks
                    coef = hop * (sums[1] + (here + end) * sums[2] + cubic * sums[3])
                else:
                    here = local(0, 0, 0)
                    degree = links(column, planes * ns) + links(row, ny) + links(lane, nz)
                    near = local(1, 0, 0) + local(-1, 0, 0) + local(0, 1, 0) + local(0, -1, 0)
                    near = near + jnp.where(lane + 1 < nz, local(0, 0, 1), 0.0)
                    near = near + jnp.where(lane >= 1, local(0, 0, -1), 0.0)
                    square = here * here + hop**2 * degree
                    cube = here * (here * here + 2.0 * hop**2 * degree) + hop**2 * near
                    coef = 0.5 * (sums[0] + here * sums[1] + square * sums[2] + cube * sums[3])
                coefs[x, index] = coef
        return carry

    lax.fori_loop(0, planes, one_plane, 0)
    when(s < ns - 1, lambda: down[1].wait_recv())

    def rho_copy(peer):
        return remote(dens.at[peer], rho_in.at[t], rho_s.at[peer], rho_r.at[t], trial=peer)

    def send(x):
        for h in range(span):
            peer = x * span + h
            when(peer != t, lambda: rho_copy(peer).start())

    def plane_at(step):
        return lax.rem(t // span + 1 + step, planes)

    def densities(step, carry):
        x = plane_at(step)

        def one_trial(k, carry):
            density = 0.0
            for dz in range(-REACH, REACH + 1):
                group = [(n, off) for n, off in enumerate(OFFSETS) if off[2] == dz]
                if not group:
                    continue
                part = 0.0
                for index, (dx, dy, _) in group:
                    part = part + coefs[x, index] * wide[k, x + dx, 8 + dy : 8 + dy + half, :]
                density = density + rolled(part, -dz)
            for h in range(span):
                dens[x * span + h, k] = density[h * piece : (h + 1) * piece]
            return carry

        lax.fori_loop(0, per, one_trial, 0)
        when(step > 0, lambda: send(plane_at(step - 1)))
        return carry

    lax.fori_loop(0, planes, densities, 0)
    send(plane_at(planes - 1))

    rho_in[t] = dens[t]
    own_tri.wait()
    for copy in tri_copies:
        copy.wait_recv()
    for j in range(1, nt):
        source = lax.rem(t + j, nt)
        remote(dens.at[source], rho_in.at[source], rho_s.at[source], rho_r.at[source], trial=source).wait_recv()

    contract = (((1,), (1,)), ((), ()))

    def dot(a, b):
        return lax.dot_general(a, b, contract, precision=HIGH, preferred_element_type=jnp.float32)

    gram = jnp.zeros((total, total), jnp.float32)
    for r in range(piece):
        left = tri_in[:, :, r, :].reshape(total, nz)
        right = rho_in[:, :, r, :].reshape(total, nz)
        gram = gram + dot(left, right) + dot(right, left)
    pick = (picks[...] == lax.broadcasted_iota(jnp.int32, (total, total), 0)).astype(jnp.float32)
    half_way = lax.dot_general(
        pick, gram, (((0,), (0,)), ((), ())), precision=HIGH, preferred_element_type=jnp.float32
    )
    factor = 1.0 / jnp.sqrt(jnp.float32(planes * ns * ny * nz * norb))
    final = jnp.dot(half_way, pick, precision=HIGH, preferred_element_type=jnp.float32) * factor
    owned = total // (nt * ns)
    for r in range(nt * ns):
        rows_out[r] = final[r * owned : (r + 1) * owned]

    def me():
        return (t * ns + s) * nf + f

    def row_copy(k):
        pt, ps, pf = device(k)
        return remote(
            rows_out.at[pt * ns + ps], rows_in.at[me()], row_s.at[k], row_r.at[k], trial=pt, slab=ps, freq=pf
        )

    def each(action):
        if count <= 64:
            for k in range(1, count):
                action(k)
        else:
            pl.loop(1, count)(action)

    each(lambda k: row_copy(k).start())
    rows_in[me()] = rows_out[t * ns + s]
    each(lambda k: row_copy(k).wait())
    out[...] = jnp.sum(rows_in[...], axis=0)

    for j in range(1, nt):
        rho_copy(lax.rem(t + j, nt)).wait_send()
    for copy in par_copies + tri_copies:
        copy.wait_send()
    for part in range(2):
        first = own if part == 0 else None
        when(can_rise, lambda: from_below(1, part, first).wait_send())
        when(can_sink, lambda: from_above(1, part, first).wait_send())
        handed(0, part, first).wait_send()
        for j in range(1, chips):
            if j + 1 < chips:
                when(can_rise & (z >= j), lambda: from_below(j + 1, part).wait_send())
                when(can_sink & (z + j < chips), lambda: from_above(j + 1, part).wait_send())
            when(z >= j, lambda: handed(-j, part).wait_send())
            when(z + j < chips, lambda: handed(j, part).wait_send())

    @pl.when(s > 0)
    def _():
        for copy in down:
            copy.wait_send()

    when(s < ns - 1, lambda: lift.wait_send())


def local(sizes, orbitals, energies, potential, trials, cheb, shifts, column_order):
    nt, ns, nf = sizes
    per, planes, ny, nz = trials.shape
    norb = orbitals.shape[0] * nt
    half = ny // nf
    full = half + 16
    total = nt * per
    piece = planes * half // nt
    owned = total // (nt * ns)
    count = nt * ns * nf
    chips = nt // 2
    column = jnp.concatenate([energies, cheb[0], shifts, jnp.zeros((2,), jnp.float32)])
    par = jnp.broadcast_to(column[:, None], (8, 128))
    f32 = jnp.float32
    dma = pltpu.SemaphoreType.DMA
    anywhere = pl.BlockSpec(memory_space=pltpu.HBM)
    vmem = pl.BlockSpec(memory_space=pltpu.VMEM)
    return pl.pallas_call(
        functools.partial(kernel, sizes),
        out_shape=jax.ShapeDtypeStruct((owned, total), f32),
        in_specs=[anywhere, vmem, anywhere, anywhere, anywhere],
        out_specs=vmem,
        scratch_shapes=[
            pltpu.VMEM((norb, planes + REACH, full, nz), f32),
            pltpu.VMEM((per, planes + REACH, full, nz), f32),
            pltpu.VMEM((planes + REACH + 1, full, nz), f32),
            pltpu.VMEM((nt, 8, 128), f32),
            pltpu.VMEM((nf, 8, 128), f32),
            pltpu.VMEM((4, norb, half, nz), f32),
            pltpu.VMEM((4, norb, 8, nz), f32),
            pltpu.VMEM((planes, len(OFFSETS), half, nz), f32),
            pltpu.VMEM((nt, per, piece, nz), f32),
            pltpu.VMEM((nt, per, piece, nz), f32),
            pltpu.VMEM((nt, per, piece, nz), f32),
            pltpu.VMEM((nt * ns, owned, total), f32),
            pltpu.VMEM((count, owned, total), f32),
            dma((4,)), dma((4,)), dma((chips, 2)), dma((chips, 2)), dma((chips, 2)), dma((chips, 2)),
            dma((2 * chips, 2)), dma((2 * chips, 2)), dma((nt,)), dma((nt,)), dma((nf,)), dma((nf,)), dma((nt,)), dma((nt,)), dma((nt,)), dma((nt,)), dma((count,)), dma((count,)),
            dma((7,)),
            pltpu.VMEM((1, total), jnp.int32),
        ],
        compiler_params=pltpu.CompilerParams(
            collective_id=0, has_side_effects=True, vmem_limit_bytes=67043328 - 65536
        ),
    )(orbitals, par, potential, trials, column_order[None])


def solution(mesh):
    sizes = tuple(mesh.shape[name] for name in ("trial", "slab", "freq"))
    in_specs = (
        P("trial", "slab", None, None),
        P("trial"),
        P("slab", None, None),
        P("trial", "slab", None, None),
        P("freq", None),
        P("freq"),
        P(),
    )
    out_specs = P(("trial", "slab"), None)
    return jax.shard_map(
        functools.partial(local, sizes), mesh=mesh, in_specs=in_specs, out_specs=out_specs, check_vma=False
    )
```
